256 devices in a mesh: req: 4 (over y), blk: 16 (over z, x_lo), tp: 4 (over x_hi, core).
Axes of the slice: x: 4 (x_hi: 2, x_lo: 2; x = x_hi * 2 + x_lo), y: 4, z: 8, core: 2. Of those that a mesh axis runs over, the one named last changes fastest.
Arguments:
- tokens: bfloat16 [4, 2048, 5120], P('req', 'blk', 'tp'), may hold values from -6 to 6
- gain: bfloat16 [5120], replicated, may hold values from 0.5 to 1.5
- w_query: bfloat16 [5120, 5120], P('req', 'tp'), may hold values from -0.078125 to 0.078125
- b_query: bfloat16 [5120], P('tp'), may hold values from -4 to 4
- w_keyval: bfloat16 [5120, 2, 1024], P('req', None, 'tp'), may hold values from -0.078125 to 0.078125
- b_keyval: bfloat16 [2, 1024], P(None, 'tp'), may hold values from -3 to 3
- kv_cache: bfloat16 [4, 2, 112, 128, 1024], P('req', None, 'blk', None, 'tp'), may hold values from -400 to 400
- cached_pages: int32 [4], P('req'), may hold values from 1 to 64, as said below
- page_table: int32 [4, 80], P('req'), may hold values from -1 to 111, as said below
Outputs:
- attended: bfloat16 [4, 2048, 5120], P('req', 'blk', 'tp')
- new_cache: bfloat16 [4, 2, 112, 128, 1024], P('req', None, 'blk', None, 'tp')
The draws below stay inside these ranges and needn't reach their ends.
Inputs may be any that keep to these rules, and one draw needn't show every extreme that they name: `cached_pages`: one request has the most, 64. `page_table`: entry p of a request's row is the slot (owner index of blk times 7 plus slot) of its logical page p for p below its cached pages plus 16, and -1 beyond; the live pages of a request use distinct slots; one index of blk holds at most 4 cached pages of a request; the request with 64 cached pages has exactly 4 on every index of blk.
All inputs are finite; a program needn't handle non-finite values.
Results may differ from the reference program's by a relative error of at most 0.012.
The reference program's roundings to bfloat16 on the way count: a program that leaves them out, or rounds other values in their place, can miss the bound.
Values may be sent and summed in bfloat16 or wider, within the bound.
A program may use at most 128 MiB of HBM per device.

```python
import jax
import jax.numpy as jnp
from jax import lax

D = 5120
QUERY_HEADS = 40
KEYVALUE_HEADS = 8
HEAD_SIZE = 128
PAGE_TOKENS = 128
CPD = 4
QW = 5120
KEY_FEATURES = 1024
SLOTS = 7
POOL = 112
NEW_TOKEN_COUNT = 2048
MOST_CACHE_PAGES = 64
NPR = 16
PT = 80
GROUPS = 4
N_BLK = 16


def slot_order(subkey):
    return jax.random.permutation(subkey, SLOTS)


def plan_group(group_key, length):
    slot_key, first_key, order_key, free_key = jax.random.split(group_key, 4)
    orders = jax.vmap(slot_order)(jax.random.split(slot_key, N_BLK)).astype(jnp.int32)
    devices = jnp.arange(N_BLK, dtype=jnp.int32)[:, None]
    held = devices * SLOTS + orders[:, :CPD]
    spare = devices * SLOTS + orders[:, CPD:]
    leader = jax.random.randint(first_key, (), 0, N_BLK)
    shuffled = jax.random.permutation(order_key, N_BLK * CPD).astype(jnp.int32).reshape(N_BLK, CPD)
    ranks = jnp.where(devices == leader, jnp.arange(CPD, dtype=jnp.int32)[None, :] - CPD, shuffled)
    cached_list = held.reshape(-1)[jnp.argsort(ranks.reshape(-1))]
    fresh_list = spare.reshape(-1)[jax.random.permutation(free_key, N_BLK * (SLOTS - CPD))][:NPR]
    pages = jnp.arange(PT, dtype=jnp.int32)
    from_cache = cached_list[jnp.clip(pages, 0, MOST_CACHE_PAGES - 1)]
    from_fresh = fresh_list[jnp.clip(pages - length, 0, NPR - 1)]
    return jnp.where(pages < length, from_cache, jnp.where(pages < length + NPR, from_fresh, -1)).astype(jnp.int32)


def plan(key):
    base_key = jax.random.fold_in(key, 101)
    pick_key, length_key, group_key = jax.random.split(base_key, 3)
    chosen = jax.random.randint(pick_key, (), 0, GROUPS)
    lengths = jax.random.randint(length_key, (GROUPS,), 1, MOST_CACHE_PAGES + 1)
    lengths = jnp.where(jnp.arange(GROUPS) == chosen, MOST_CACHE_PAGES, lengths).astype(jnp.int32)
    tables = jax.vmap(plan_group)(jax.random.split(group_key, GROUPS), lengths)
    return (lengths, tables)


def draw_cached_pages(key, part):
    return plan(key)[0]


def draw_page_table(key, part):
    return plan(key)[1]


def bias_start(key):
    return jnp.clip(jax.random.normal(jax.random.fold_in(key, 202), (QW,), jnp.float32), -4.0, 4.0)


def draw_b_query(key, part):
    rotary_base = bias_start(key)
    result = 0.5 * rotary_base
    return result.astype(jnp.bfloat16)


def draw_kv_cache(key, part):
    shape = (GROUPS, 2, POOL, PAGE_TOKENS, KEY_FEATURES)
    noise_key = jax.random.fold_in(key, 303)
    result = jax.random.normal(noise_key, shape, jnp.float32)
    return result.astype(jnp.bfloat16)


def block_levels(key, shape, shards, low, top_value):
    factor_of = 1.0
    for dim, parts in shards:
        heights = jax.random.uniform(jax.random.fold_in(jax.random.fold_in(key, 6), dim), (parts,), jnp.float32, low / len(shards), top_value / len(shards))
        factor_of = factor_of * jnp.repeat(jnp.exp(heights), shape[dim] // parts).reshape((-1,) + (1,) * (len(shape) - 1 - dim))
    return factor_of


def centred(rng, extent, scale, reach, pieces=(), held_as=jnp.bfloat16):
    factor_of = block_levels(rng, extent, pieces, -0.22, 0.18) if pieces else 1.0
    values = jax.random.normal(rng, extent, jnp.float32) * scale * factor_of
    return jnp.minimum(jnp.maximum(values, -reach), reach).astype(held_as)


def setup_inputs(seed: int = 0) -> dict:
    streams_of = jax.random.split(jax.random.key(seed), 10)
    tokens = centred(streams_of[0], (GROUPS, NEW_TOKEN_COUNT, D), 1.0, 6.0, ((0, 4), (1, 16), (2, 4)))
    gain = jnp.clip(1.0 + 0.1 * jax.random.normal(streams_of[1], (D,), jnp.float32), 0.5, 1.5).astype(jnp.bfloat16)
    w_query = centred(streams_of[2], (D, QW), D ** -0.5, 0.078125, ((0, 4), (1, 4)))
    b_query = draw_b_query(jax.random.fold_in(streams_of[9], 71), 0)
    w_keyval = centred(streams_of[4], (D, 2, KEY_FEATURES), D ** -0.5, 0.078125, ((0, 4), (2, 4)))
    b_keyval = centred(streams_of[5], (2, KEY_FEATURES), 0.5, 3.0, ((1, 4),))
    kv_cache = draw_kv_cache(jax.random.fold_in(streams_of[9], 71), 0)
    cached_pages = draw_cached_pages(jax.random.fold_in(streams_of[9], 71), 0)
    page_table = draw_page_table(jax.random.fold_in(streams_of[9], 71), 0)
    return {"tokens": tokens, "gain": gain, "w_query": w_query, "b_query": b_query, "w_keyval": w_keyval, "b_keyval": b_keyval, "kv_cache": kv_cache, "cached_pages": cached_pages, "page_table": page_table}


epsilon = 1e-06
rope_base = 1000000.0

def normalize(inputs, gain):
    floats = inputs.astype(jnp.float32)
    scaling = lax.rsqrt(lax.optimization_barrier(jnp.mean(floats * floats, axis=-1, keepdims=True)) + epsilon)
    return (floats * scaling * gain.astype(jnp.float32)).astype(jnp.bfloat16)

def apply_rotation(vectors, token_positions):
    halfway = vectors.shape[-1] // 2
    frequency = rope_base ** (-(jnp.arange(halfway, dtype=jnp.float32) * 2.0 / vectors.shape[-1]))
    angles = token_positions[:, None] * frequency[None, :]
    cosine = jnp.cos(angles)[:, None, :]
    sine_part = jnp.sin(angles)[:, None, :]
    leading = vectors[..., :halfway]
    trailing = vectors[..., halfway:]
    return jnp.concatenate([leading * cosine - trailing * sine_part, trailing * cosine + leading * sine_part], axis=-1)

def head_attention(operands):
    query_rows_all, key_rows, value_rows, allowed = operands
    scaling = HEAD_SIZE ** (-0.5)
    scores = jnp.einsum('rjd,kd->rjk', query_rows_all.astype(jnp.float32), key_rows.astype(jnp.float32)) * scaling
    scores = jnp.where(allowed[:, None, :], scores, -jnp.inf)
    maxima = lax.optimization_barrier(jnp.max(scores, axis=-1, keepdims=True))
    weights = jnp.exp(scores - maxima)
    totals = lax.optimization_barrier(jnp.sum(weights, axis=-1))
    rounded = lax.optimization_barrier(weights.astype(jnp.bfloat16))
    blended = jnp.einsum('rjk,kd->rjd', rounded.astype(jnp.float32), value_rows.astype(jnp.float32))
    return blended / totals[..., None]

def reference(tokens, gain, w_query, b_query, w_keyval, b_keyval, kv_cache, cached_pages, page_table):
    queries_per_group = QUERY_HEADS // KEYVALUE_HEADS
    attended_all = []
    caches_all = []
    for request in range(GROUPS):
        normed = normalize(tokens[request], gain)
        query_raw = jnp.dot(normed, w_query, preferred_element_type=jnp.float32) + b_query.astype(jnp.float32)
        key_value_pairs = jnp.dot(normed, w_keyval.reshape(D, 2 * KEY_FEATURES), preferred_element_type=jnp.float32) + b_keyval.reshape(2 * KEY_FEATURES).astype(jnp.float32)
        length = cached_pages[request]
        token_positions = (length * PAGE_TOKENS + jnp.arange(NEW_TOKEN_COUNT, dtype=jnp.int32)).astype(jnp.float32)
        query_rows_all = apply_rotation(query_raw.reshape(NEW_TOKEN_COUNT, QUERY_HEADS, HEAD_SIZE), token_positions).astype(jnp.bfloat16)
        incoming_keys = apply_rotation(key_value_pairs[:, :KEY_FEATURES].reshape(NEW_TOKEN_COUNT, KEYVALUE_HEADS, HEAD_SIZE), token_positions).astype(jnp.bfloat16)
        incoming_values = key_value_pairs[:, KEY_FEATURES:].reshape(NEW_TOKEN_COUNT, KEYVALUE_HEADS, HEAD_SIZE).astype(jnp.bfloat16)
        page_map = page_table[request]
        cache_storage = kv_cache[request]
        cache_slot_index = jnp.clip(page_map[:MOST_CACHE_PAGES], 0, POOL - 1)
        stored_tokens = cache_storage[:, cache_slot_index].reshape(2, MOST_CACHE_PAGES * PAGE_TOKENS, KEYVALUE_HEADS, HEAD_SIZE)
        all_keys = jnp.concatenate([stored_tokens[0], incoming_keys], axis=0)
        all_values = jnp.concatenate([stored_tokens[1], incoming_values], axis=0)
        cached_valid = jnp.arange(MOST_CACHE_PAGES * PAGE_TOKENS, dtype=jnp.int32) // PAGE_TOKENS < length
        causal = jnp.arange(NEW_TOKEN_COUNT, dtype=jnp.int32)[None, :] <= jnp.arange(NEW_TOKEN_COUNT, dtype=jnp.int32)[:, None]
        allowed = jnp.concatenate([jnp.broadcast_to(cached_valid[None, :], (NEW_TOKEN_COUNT, MOST_CACHE_PAGES * PAGE_TOKENS)), causal], axis=1)
        grouped_queries = query_rows_all.reshape(NEW_TOKEN_COUNT, KEYVALUE_HEADS, queries_per_group, HEAD_SIZE).transpose(1, 0, 2, 3)
        per_head = lax.map(lambda operands: head_attention((operands[0], operands[1], operands[2], allowed)), (grouped_queries, all_keys.transpose(1, 0, 2), all_values.transpose(1, 0, 2)))
        attended = per_head.transpose(1, 0, 2, 3).reshape(NEW_TOKEN_COUNT, QW).astype(jnp.bfloat16)
        fresh_pages = jnp.stack([incoming_keys.reshape(NEW_TOKEN_COUNT, KEY_FEATURES), incoming_values.reshape(NEW_TOKEN_COUNT, KEY_FEATURES)]).reshape(2, NPR, PAGE_TOKENS, KEY_FEATURES)
        new_slots = lax.dynamic_slice(page_map, (length.astype(jnp.int32),), (NPR,))
        attended_all.append(attended)
        caches_all.append(cache_storage.at[:, new_slots].set(fresh_pages))
    return (jnp.stack(attended_all), jnp.stack(caches_all))
```

```python
import functools

import jax
import jax.numpy as jnp
from jax import lax
from jax.experimental import pallas as pl
from jax.experimental.pallas import tpu as pltpu
from jax.sharding import PartitionSpec as P

HEAD = 128
PAGE = 128
SLOTS = 7
CPD = 4
EPS = 1e-06
ROPE_BASE = 1000000.0
LOG2E = 1.4426950408889634
NEG = -1e30
MESH = pl.DeviceIdType.MESH


def kernel(
    sel_ref, new_idx_ref, new_land_ref,
    tok_hbm, gain_ref, wq_hbm, wkv_hbm, bias_ref, cos_ref, sin_ref, mask_ref, kv_hbm,
    out_ref, cache_out,
    tok_all, nrm, xr, w_ref, part, ring, kv_own, kv_all, fr_all, q_ref, m_ref, l_ref, acc_ref,
    loc_sem, a_send, a_recv, y_send, y_recv, ys_send, ys_recv, b_send, b_recv,
    kz_send, kz_recv, kx_send, kx_recv, fz_send, fz_recv, fx_send, fx_recv,
):
    r = lax.axis_index("req")
    b = lax.axis_index("blk")
    t = lax.axis_index("tp")
    z, xl = b // 2, b % 2
    core = t % 2
    sib = t + 1 - 2 * core
    far = (t + 2) % 4
    sib_far = (sib + 2) % 4
    pair = b + 1 - 2 * xl
    chunk = tok_hbm.shape[1]
    rows = tok_hbm.shape[0]
    half = rows // 2
    started = []

    def at_z(delta):
        return ((z + delta + 8) % 8) * 2 + xl

    def copy(src, dst, send, recv, **device):
        return pltpu.make_async_remote_copy(
            src_ref=src, dst_ref=dst, send_sem=send, recv_sem=recv,
            device_id=device, device_id_type=MESH,
        )

    def send(src, dst, send_sem, recv_sem, **device):
        c = copy(src, dst, send_sem, recv_sem, **device)
        c.start()
        started.append(c)

    def await_recv(dst, send_sem, recv_sem, **device):
        copy(dst, dst, send_sem, recv_sem, **device).wait_recv()

    tok_in = pltpu.make_async_copy(tok_hbm, tok_all.at[t], loc_sem.at[0])
    tok_in.start()
    kv_in = pltpu.make_async_copy(kv_hbm, kv_own, loc_sem.at[1])
    kv_in.start()
    w_in = [
        pltpu.make_async_copy(wkv_hbm.at[:, 0:256], w_ref.at[:, 0:256], loc_sem.at[2]),
        pltpu.make_async_copy(wq_hbm.at[:, 0:640], w_ref.at[:, 256:896], loc_sem.at[3]),
        pltpu.make_async_copy(wkv_hbm.at[:, 256:512], w_ref.at[:, 896:1152], loc_sem.at[4]),
        pltpu.make_async_copy(wq_hbm.at[:, 640:1280], w_ref.at[:, 1152:1792], loc_sem.at[5]),
    ]
    for c in w_in:
        c.start()

    barrier = pltpu.get_barrier_semaphore()
    peers = [dict(tp=sib), dict(tp=far), dict(blk=pair), dict(blk=at_z(1)), dict(blk=at_z(-1))]
    peers += [dict(req=(r + d) % 4) for d in (1, 2, 3)]
    for peer in peers:
        pl.semaphore_signal(barrier, inc=1, device_id=peer, device_id_type=MESH)
    pl.semaphore_wait(barrier, len(peers))

    tok_in.wait()
    send(tok_all.at[t], tok_all.at[t], a_send.at[1], a_recv.at[1], tp=far)
    send(tok_all.at[t], tok_all.at[t], a_send.at[0], a_recv.at[0], tp=sib)

    kv_in.wait()
    for j in range(CPD):
        s = sel_ref[j]
        for c in range(2):
            kv_all[b, c, j * PAGE:(j + 1) * PAGE, :] = kv_own[c, s]

    def kz_region(direction, step, piece, origin):
        block = origin * 2 + (xl if piece == 0 else 1 - xl)
        size = 512 if piece == 0 else 256
        lo, n = 0, size
        if step == 3:
            n = size // 2
            lo = 0 if direction == 0 else n
        return kv_all.at[block, :, lo:lo + n, :]

    def kz_send_piece(direction, step, piece):
        sign = 1 if direction == 0 else -1
        origin = (z - sign * step + 8) % 8
        region = kz_region(direction, step, piece, origin)
        send(region, region, kz_send.at[direction, step, piece], kz_recv.at[direction, step, piece],
             blk=at_z(sign))

    def kz_await(direction, step, piece):
        sign = 1 if direction == 0 else -1
        origin = (z - sign * (step + 1) + 8) % 8
        region = kz_region(direction, step, piece, origin)
        await_recv(region, kz_send.at[direction, step, piece], kz_recv.at[direction, step, piece],
                   blk=at_z(sign))
        return origin

    def kx_send_tail(origin, k):
        region = kv_all.at[origin * 2 + xl, :, 256:512, :]
        send(region, region, kx_send.at[k], kx_recv.at[k], blk=pair)

    def kx_await_tail(origin, k):
        region = kv_all.at[origin * 2 + 1 - xl, :, 256:512, :]
        await_recv(region, kx_send.at[k], kx_recv.at[k], blk=pair)

    tails = []

    def kv_advance(step):
        for piece in range(2):
            for direction in range(2):
                origin = kz_await(direction, step, piece)
                if step < 3:
                    kz_send_piece(direction, step + 1, piece)
                if piece == 0 and (step < 3 or direction == 1):
                    tails.append(origin)
                    kx_send_tail(origin, len(tails))

    for direction in range(2):
        kz_send_piece(direction, 0, 0)

    await_recv(tok_all.at[far], a_send.at[1], a_recv.at[1], tp=far)
    send(tok_all.at[far], tok_all.at[far], a_send.at[2], a_recv.at[2], tp=sib)
    head_rows = kv_all.at[b, :, 0:256, :]
    send(head_rows, head_rows, kx_send.at[8], kx_recv.at[8], blk=pair)
    kx_send_tail(z, 0)
    await_recv(tok_all.at[sib], a_send.at[0], a_recv.at[0], tp=sib)
    await_recv(tok_all.at[sib_far], a_send.at[2], a_recv.at[2], tp=sib)

    total = jnp.zeros((rows, 1), jnp.float32)
    for c in range(4):
        x = tok_all[c].astype(jnp.float32)
        total = total + jnp.sum(x * x, axis=1, keepdims=True)
    scaling = lax.rsqrt(total / (4 * chunk) + EPS)
    for c in range(4):
        x = tok_all[c].astype(jnp.float32)
        nrm[c] = (x * scaling * gain_ref[:, c * chunk:(c + 1) * chunk]).astype(jnp.bfloat16)

    def y_half(c):
        return pl.ds(c * half, half)

    for d in (2, 1, 3):
        dest = (r + d) % 4
        mine = pl.ds(pl.multiple_of(core * half, half), half)
        send(nrm.at[dest, mine], xr.at[r, mine], y_send.at[d - 1], y_recv.at[d - 1], req=dest)

    for c in w_in:
        c.wait()

    tiles = w_ref.shape[1] // 256

    def project(slot, lhs_of):
        def tile(i, carry):
            cols = pl.ds(pl.multiple_of(i * 256, 256), 256)
            part[slot, :, cols] = jnp.dot(lhs_of(), w_ref[:, cols], preferred_element_type=jnp.float32)
            return carry

        lax.fori_loop(0, tiles, tile, 0)

    project(r, lambda: nrm[r])

    await_recv(kv_all.at[pair, :, 0:256, :], kx_send.at[8], kx_recv.at[8], blk=pair)
    for direction in range(2):
        kz_send_piece(direction, 0, 1)

    mine = pl.ds(pl.multiple_of(core * half, half), half)
    other = pl.ds(pl.multiple_of((1 - core) * half, half), half)
    for d in (1, 3, 2):
        origin = (r + 4 - d) % 4
        await_recv(xr.at[origin, mine], y_send.at[d - 1], y_recv.at[d - 1], req=(r + d) % 4)
        send(xr.at[origin, mine], xr.at[origin, mine], ys_send.at[d - 1], ys_recv.at[d - 1], tp=sib)

    spans = ((0, 256), (256, 640))

    def b_send_piece(direction, step, piece):
        sign = 1 if direction == 0 else -1
        dest = (r + 4 - sign * (step + 1)) % 4
        lo = direction * 896 + spans[piece][0]
        n = spans[piece][1]
        src = part.at[dest, :, lo:lo + n]
        dst = ring.at[step, :, lo:lo + n]
        send(src, dst, b_send.at[direction, step, piece], b_recv.at[direction, step, piece],
             req=(r + 4 + sign) % 4)

    def b_take(direction, step, piece):
        sign = 1 if direction == 0 else -1
        dest = (r + 4 - sign * (step + 2)) % 4
        lo = direction * 896 + spans[piece][0]
        n = spans[piece][1]
        await_recv(ring.at[step, :, lo:lo + n], b_send.at[direction, step, piece],
                   b_recv.at[direction, step, piece], req=(r + 4 + sign) % 4)
        part[dest, :, lo:lo + n] += ring[step, :, lo:lo + n]

    for d in (1, 3, 2):
        origin = (r + 4 - d) % 4
        await_recv(xr.at[origin, other], ys_send.at[d - 1], ys_recv.at[d - 1], tp=sib)
        project(origin, lambda: xr[origin])
        if d == 1:
            for piece in range(2):
                b_send_piece(0, 0, piece)
        if d == 3:
            for piece in range(2):
                b_send_piece(1, 0, piece)

    kv_advance(0)
    for step in range(2):
        for piece in range(2):
            for direction in range(2):
                b_take(direction, step, piece)
                b_send_piece(direction, step + 1, piece)
        kv_advance(step + 1)

    def rotate(v):
        return v * cos_ref[...] + pltpu.roll(v, 64, 1) * sin_ref[...]

    def fresh_page(block):
        return fr_all.at[block]

    def fz_block(origin, piece):
        return origin * 2 + (xl if piece == 0 else 1 - xl)

    def fz_send_piece(direction, step, piece):
        sign = 1 if direction == 0 else -1
        origin = (z - sign * step + 8) % 8
        region = fresh_page(fz_block(origin, piece))
        send(region, region, fz_send.at[direction, step, piece], fz_recv.at[direction, step, piece],
             blk=at_z(sign))

    def fz_await(direction, step, piece):
        sign = 1 if direction == 0 else -1
        origin = (z - sign * (step + 1) + 8) % 8
        region = fresh_page(fz_block(origin, piece))
        await_recv(region, fz_send.at[direction, step, piece], fz_recv.at[direction, step, piece],
                   blk=at_z(sign))

    for direction in range(2):
        b_take(direction, 2, 0)
    for h in range(2):
        k = part[r, :, h * HEAD:(h + 1) * HEAD] + bias_ref[:, h * HEAD:(h + 1) * HEAD]
        fr_all[b, 0, :, h * HEAD:(h + 1) * HEAD] = rotate(k).astype(jnp.bfloat16)
    fr_all[b, 1, :, :] = (part[r, :, 896:1152] + bias_ref[:, 896:1152]).astype(jnp.bfloat16)
    send(fresh_page(b), fresh_page(b), fx_send, fx_recv, blk=pair)
    for direction in range(2):
        fz_send_piece(direction, 0, 0)
    for direction in range(2):
        b_take(direction, 2, 1)
    for h in range(2):
        for j in range(5):
            lo = h * 896 + 256 + j * HEAD
            q = part[r, :, lo:lo + HEAD] + bias_ref[:, lo:lo + HEAD]
            q_ref[h, j * rows:(j + 1) * rows, :] = rotate(q).astype(jnp.bfloat16)

    kv_advance(3)
    kx_await_tail(z, 0)
    for k, origin in enumerate(tails):
        kx_await_tail(origin, k + 1)

    m_ref[...] = jnp.full(m_ref.shape, NEG, jnp.float32)
    l_ref[...] = jnp.zeros(l_ref.shape, jnp.float32)
    acc_ref[...] = jnp.zeros(acc_ref.shape, jnp.float32)
    factor = HEAD ** (-0.5) * LOG2E

    def attend(h, k, v, adjust):
        s = lax.dot_general(q_ref[h], k, (((1,), (1,)), ((), ())), preferred_element_type=jnp.float32)
        s = adjust(s * factor)
        m_old = m_ref[h]
        m_new = jnp.maximum(m_old, jnp.max(s, axis=1, keepdims=True))
        p = jnp.exp2(s - m_new)
        decay = jnp.exp2(m_old - m_new)
        m_ref[h] = m_new
        l_ref[h] = l_ref[h] * decay + jnp.sum(p, axis=1, keepdims=True)
        acc_ref[h] = acc_ref[h] * decay + jnp.dot(
            p.astype(jnp.bfloat16), v, preferred_element_type=jnp.float32
        )

    def cached_block(i, carry):
        bias_row = mask_ref[i]
        for h in range(2):
            cols = slice(h * HEAD, (h + 1) * HEAD)
            attend(h, kv_all[i, 0, :, cols], kv_all[i, 1, :, cols], lambda s: s + bias_row)
        return carry

    def cached(lo, hi):
        lax.fori_loop(lo, hi, cached_block, 0)

    cached(0, 3)
    await_recv(fresh_page(pair), fx_send, fx_recv, blk=pair)
    for direction in range(2):
        fz_send_piece(direction, 0, 1)
    cached(3, 5)
    done = 5
    for step in range(4):
        for piece in range(2):
            for direction in range(2):
                if step == 3 and piece != direction:
                    continue
                fz_await(direction, step, piece)
                if step < 2 or (step == 2 and piece == direction):
                    fz_send_piece(direction, step + 1, piece)
            if step < 3:
                upto = min(done + 2, 16)
                cached(done, upto)
                done = upto
    if done < 16:
        cached(done, 16)

    for s in range(SLOTS):
        i = new_idx_ref[s]
        land = jnp.broadcast_to(new_land_ref[s], (PAGE, 256)) > 0
        for c in range(2):
            kv_own[c, s] = jnp.where(land, fr_all[i, c], kv_own[c, s])
    cache_copy = pltpu.make_async_copy(kv_own, cache_out, loc_sem.at[6])
    cache_copy.start()

    def fresh_pair(i, carry):
        for h in range(2):
            cols = slice(h * HEAD, (h + 1) * HEAD)
            k = jnp.concatenate([fr_all[2 * i, 0, :, cols], fr_all[2 * i + 1, 0, :, cols]], axis=0)
            v = jnp.concatenate([fr_all[2 * i, 1, :, cols], fr_all[2 * i + 1, 1, :, cols]], axis=0)
            attend(h, k, v, lambda s: s)
        return carry

    lax.fori_loop(0, z, fresh_pair, 0)
    shape = (5 * rows, 2 * PAGE)
    token = lax.broadcasted_iota(jnp.int32, shape, 0) % rows + xl * rows
    allowed = lax.broadcasted_iota(jnp.int32, shape, 1) <= token
    for h in range(2):
        cols = slice(h * HEAD, (h + 1) * HEAD)
        k = jnp.concatenate([fr_all[2 * z, 0, :, cols], fr_all[2 * z + 1, 0, :, cols]], axis=0)
        v = jnp.concatenate([fr_all[2 * z, 1, :, cols], fr_all[2 * z + 1, 1, :, cols]], axis=0)
        attend(h, k, v, lambda s: jnp.where(allowed, s, NEG))

    for h in range(2):
        for j in range(5):
            lo = (h * 5 + j) * HEAD
            span = slice(j * rows, (j + 1) * rows)
            out_ref[:, lo:lo + HEAD] = (acc_ref[h, span] / l_ref[h, span]).astype(jnp.bfloat16)

    cache_copy.wait()
    for c in started:
        c.wait_send()


def body(tokens, gain, w_query, b_query, w_keyval, b_keyval, kv_cache, cached_pages, page_table):
    rows, chunk = tokens.shape[1], tokens.shape[2]
    query_width = w_query.shape[1]
    kv_width = w_keyval.shape[2]
    n_blk = lax.axis_size("blk")
    b = lax.axis_index("blk")
    length = cached_pages[0]
    page_map = page_table[0]
    slot_ids = jnp.arange(n_blk * SLOTS, dtype=jnp.int32)
    live = jnp.arange(page_map.shape[0], dtype=jnp.int32) < length
    valid = jnp.any((page_map[None, :] == slot_ids[:, None]) & live[None, :], axis=1)
    valid = valid.reshape(n_blk, SLOTS)
    counts = jnp.sum(valid.astype(jnp.int32), axis=1)
    mask = jnp.where(
        jnp.arange(CPD * PAGE, dtype=jnp.int32)[None, :] // PAGE < counts[:, None], 0.0, NEG
    ).astype(jnp.float32)[:, None, :]
    own = lax.dynamic_slice_in_dim(valid, b, 1, 0)[0].astype(jnp.int32)
    slots = jnp.arange(SLOTS, dtype=jnp.int32)
    before = jnp.sum(own[None, :] * (slots[None, :] < slots[:, None]).astype(jnp.int32), axis=1)
    picks = jnp.arange(CPD, dtype=jnp.int32)
    sel = jnp.sum(
        slots[None, :] * ((before[None, :] == picks[:, None]) & (own[None, :] > 0)).astype(jnp.int32), axis=1
    )
    new_slots = lax.dynamic_slice_in_dim(page_map, length, n_blk)
    chooser = new_slots[None, :] == b * SLOTS + slots[:, None]
    new_idx = jnp.sum(jnp.arange(n_blk, dtype=jnp.int32)[None, :] * chooser.astype(jnp.int32), axis=1)
    new_land = jnp.any(chooser, axis=1).astype(jnp.int32)

    half_head = HEAD // 2
    frequency = ROPE_BASE ** (-(jnp.arange(half_head, dtype=jnp.float32) * 2.0 / HEAD))
    token_index = b * rows + jnp.arange(rows, dtype=jnp.int32)
    angles = (length * PAGE + token_index).astype(jnp.float32)[:, None] * frequency[None, :]
    cosine, sine = jnp.cos(angles), jnp.sin(angles)
    cos_full = jnp.concatenate([cosine, cosine], axis=1)
    sin_full = jnp.concatenate([-sine, sine], axis=1)

    bq = b_query.astype(jnp.float32)
    bkv = b_keyval.astype(jnp.float32)
    bias = jnp.concatenate([bkv[0], bq[:640], bkv[1], bq[640:]])[None, :]

    vmem = pl.BlockSpec(memory_space=pltpu.VMEM)
    smem = pl.BlockSpec(memory_space=pltpu.SMEM)
    hbm = pl.BlockSpec(memory_space=pl.ANY)
    bf, f32 = jnp.bfloat16, jnp.float32
    dma = pltpu.SemaphoreType.DMA
    width = query_width + 2 * kv_width
    attended, new_cache = pl.pallas_call(
        kernel,
        out_shape=(
            jax.ShapeDtypeStruct((rows, query_width), bf),
            jax.ShapeDtypeStruct(kv_cache.shape[1:], bf),
        ),
        in_specs=[smem] * 3 + [hbm, vmem, hbm, hbm, vmem, vmem, vmem, vmem, hbm],
        out_specs=(vmem, hbm),
        scratch_shapes=[
            pltpu.VMEM((4, rows, chunk), bf),
            pltpu.VMEM((4, rows, chunk), bf),
            pltpu.VMEM((4, rows, chunk), bf),
            pltpu.VMEM((chunk, width), bf),
            pltpu.VMEM((4, rows, width), f32),
            pltpu.VMEM((3, rows, width), f32),
            pltpu.VMEM(kv_cache.shape[1:], bf),
            pltpu.VMEM((n_blk, 2, CPD * PAGE, kv_width), bf),
            pltpu.VMEM((n_blk, 2, PAGE, kv_width), bf),
            pltpu.VMEM((2, 5 * rows, HEAD), bf),
            pltpu.VMEM((2, 5 * rows, 1), f32),
            pltpu.VMEM((2, 5 * rows, 1), f32),
            pltpu.VMEM((2, 5 * rows, HEAD), f32),
            dma((7,)), dma((3,)), dma((3,)), dma((3,)), dma((3,)), dma((3,)), dma((3,)),
            dma((2, 3, 2)), dma((2, 3, 2)),
            dma((2, 4, 2)), dma((2, 4, 2)), dma((9,)), dma((9,)),
            dma((2, 4, 2)), dma((2, 4, 2)), dma, dma,
        ],
        compiler_params=pltpu.CompilerParams(
            collective_id=0, has_side_effects=True, vmem_limit_bytes=60 * 1024 * 1024
        ),
    )(
        sel, new_idx, new_land,
        tokens[0], gain.astype(f32)[None, :], w_query, w_keyval.reshape(chunk, 2 * kv_width), bias,
        cos_full, sin_full, mask, kv_cache[0],
    )
    return attended[None], new_cache[None]


def solution(mesh):
    return jax.shard_map(
        body,
        mesh=mesh,
        in_specs=(
            P("req", "blk", "tp"),
            P(),
            P("req", "tp"),
            P("tp"),
            P("req", None, "tp"),
            P(None, "tp"),
            P("req", None, "blk", None, "tp"),
            P("req"),
            P("req", None),
        ),
        out_specs=(P("req", "blk", "tp"), P("req", None, "blk", None, "tp")),
        check_vma=False,
    )
```
